32 devices in a mesh: src: 8 (over z, x), dst: 4 (over y, core).
Axes of the slice: x: 2, y: 2, z: 4, core: 2. Of those that a mesh axis runs over, the one named last changes fastest.
Arguments:
- values: bfloat16 [256, 32, 128, 128], P(('src', 'dst')), may hold values from -6 to 6
- until: int32 [256, 128, 128], P(('src', 'dst')), may hold values from 0 to 32
- blocks: int32 [256, 3], P(('src', 'dst')), may hold values from 0 to 255, as said below
- count: int32 [32], P(('src', 'dst')), may hold values from 1 to 8, as said below
- a_factor: bfloat16 [64, 32768], P('dst', 'src'), may hold values from -6 to 6
- b_factor: bfloat16 [64, 16384], P('src', 'dst'), may hold values from -6 to 6
- c_factor: bfloat16 [32, 256], P(None, ('src', 'dst')), may hold values from -6 to 6
- core: float32 [64, 64, 32], replicated, may hold values from -0.0048828125 to 0.0048828125
Outputs:
- ttmc_t: float32 [64, 32768], P('dst', 'src')
The draws below stay inside these ranges and needn't reach their ends.
Inputs may be any that keep to these rules, and one draw needn't show every extreme that they name: Rows of blocks come 8 to a device, devices in the order of src then dst; the rows of device (p, q) name source blocks p * 32 to p * 32 + 31, destination blocks q * 32 to q * 32 + 31 and hour blocks below 8, no block twice on a device, and every row names such a block even where its slot is not live. `count`: entry p * 4 + q counts the live slots of device (p, q), which are its first ones; some device has all 8 live.
All inputs are finite; a program needn't handle non-finite values.
Results may differ from the reference program's by a relative error of at most 0.0003.
Values may be sent and summed in bfloat16 or wider, within the bound.
A program may use at most 128 MiB of HBM per device.

```python
import jax
import jax.numpy as jnp
from jax import lax

R1 = 64
R2 = 64
R3 = 32
BI = 128
BJ = 128
BT = 32
SB_DEV = 32
DB_DEV = 32
NTB = 8
CAP = 8
NSB = 256
NDB = 128
ROWS = 32768
COLS = 16384
HOURS = 256
SLOTS = 256
N_SRC = 8
N_DST = 4


def draw_blocks(key, part):
    devices = N_SRC * N_DST
    positions = SB_DEV * DB_DEV * NTB
    scores = jax.random.randint(jax.random.fold_in(key, 11), (devices, positions), 0, 4096)
    scores = scores * positions + jnp.arange(positions, dtype=jnp.int32)[None, :]
    device_grid = jnp.arange(devices, dtype=jnp.int32)[:, None]
    position_grid = jnp.arange(positions, dtype=jnp.int32)[None, :]
    forced = (device_grid == devices - 1) & (position_grid == positions - 1)
    scores = jnp.where(forced, jnp.full_like(scores, -1), scores)
    chosen = jnp.argsort(scores, axis=1, stable=True)[:, :CAP].astype(jnp.int32)
    device_ids = jnp.arange(devices, dtype=jnp.int32)[:, None]
    src_pos = device_ids // N_DST
    dst_pos = device_ids % N_DST
    source_block = src_pos * SB_DEV + chosen // (DB_DEV * NTB)
    target_block = dst_pos * DB_DEV + chosen // NTB % DB_DEV
    hour_block = chosen % NTB
    stacked = jnp.stack([source_block, target_block, hour_block], axis=-1)
    return stacked.reshape(devices * CAP, 3).astype(jnp.int32)


def draw_count(key, part):
    devices = N_SRC * N_DST
    raw_draw = jax.random.randint(jax.random.fold_in(key, 23), (devices,), 0, CAP)
    counted = 1 + raw_draw * raw_draw // CAP
    busiest = jax.random.randint(jax.random.fold_in(key, 29), (), 0, devices)
    full_cap = jnp.full((devices,), CAP, jnp.int32)
    return jnp.where(jnp.arange(devices, dtype=jnp.int32) == busiest, full_cap, counted).astype(jnp.int32)


def plant(array, stream_key, smallest, top_value):
    longest = array.shape.index(max(array.shape))
    spots = []
    for shift in (0, 1):
        where = [jax.random.randint(jax.random.fold_in(stream_key, axis), (), 0, length) for axis, length in enumerate(array.shape)]
        where[longest] = (where[longest] + shift) % array.shape[longest]
        spots.append(tuple(where))
    return array.at[spots[0]].set(smallest).at[spots[1]].set(top_value)


def levels(key, dims, pieces, smallest, largest):
    level = 1.0
    for dim, blocks in pieces:
        steps = jax.random.uniform(jax.random.fold_in(jax.random.fold_in(key, 6), dim), (blocks,), jnp.float32, smallest / len(pieces), largest / len(pieces))
        level = level * jnp.repeat(jnp.exp(steps), dims[dim] // blocks).reshape((-1,) + (1,) * (len(dims) - 1 - dim))
    return level


def bell_draw(rng, extent, spread, limit, cuts=(), kind=jnp.bfloat16):
    values = spread * jax.random.normal(rng, extent, jnp.float32)
    if cuts:
        values = values * levels(rng, extent, cuts, -0.22, 0.18)
    return jnp.clip(values, -limit, limit).astype(kind)


def setup_inputs(seed: int = 0) -> dict:
    seeds = jax.random.split(jax.random.key(seed), 9)
    values = bell_draw(seeds[0], (SLOTS, BT, BI, BJ), 1.0, 6.0, ((0, 32),))
    until = plant(jax.random.randint(seeds[1], (SLOTS, BI, BJ), 0, BT + 1), jax.random.fold_in(seeds[1], 1), 0, BT).astype(jnp.int32)
    blocks = draw_blocks(jax.random.fold_in(seeds[8], 71), 0)
    count = draw_count(jax.random.fold_in(seeds[8], 71), 0)
    a_factor = bell_draw(seeds[4], (R1, ROWS), 1.0, 6.0, ((0, 4), (1, 8)))
    b_factor = bell_draw(seeds[5], (R2, COLS), 1.0, 6.0, ((0, 8), (1, 4)))
    c_factor = bell_draw(seeds[6], (R3, HOURS), 1.0, 6.0, ((1, 32),))
    core = bell_draw(seeds[7], (R1, R2, R3), ((R2 * R3 * BJ * BT) ** -0.5), 0.0048828125, (), jnp.float32)
    return dict(values=values, until=until, blocks=blocks, count=count, a_factor=a_factor, b_factor=b_factor, c_factor=c_factor, core=core)


highest = lax.Precision.HIGHEST


def reference(values, until, blocks, count, a_factor, b_factor, c_factor, core):
    rank_a, rank_b, rank_c = core.shape
    a_wide = a_factor.astype(jnp.float32).reshape(rank_a, NSB, BI)
    b_narrow = b_factor.reshape(rank_b, NDB, BJ)
    c_wide = c_factor.astype(jnp.float32).reshape(rank_c, NTB, BT)
    slot_ids = jnp.arange(values.shape[0], dtype=jnp.int32)
    live_slots = (slot_ids % CAP) < count[slot_ids // CAP]
    hour_ids = jnp.arange(BT, dtype=jnp.int32)

    def per_block(running, item):
        block_vals, hour_limit, where_at, is_live = item
        a_rows = lax.dynamic_index_in_dim(a_wide, where_at[0], 1, keepdims=False)
        b_rows = lax.dynamic_index_in_dim(b_narrow, where_at[1], 1, keepdims=False).astype(jnp.float32)
        c_rows = lax.dynamic_index_in_dim(c_wide, where_at[2], 1, keepdims=False)
        first = jnp.einsum("abk,kt->tab", core, c_rows, precision=highest)
        second = jnp.einsum("tab,bj->atj", first, b_rows, precision=highest)
        rebuilt = jnp.einsum("ai,atj->tij", a_rows, second, precision=highest)
        observed = hour_ids[:, None, None] < hour_limit[None, :, :]
        imputed = jnp.where(observed, block_vals.astype(jnp.float32), rebuilt).astype(jnp.bfloat16)
        imputed = lax.optimization_barrier(imputed)
        along_dst = jnp.einsum("tij,bj->bti", imputed.astype(jnp.float32), b_rows, precision=highest)
        inner_sum = jnp.einsum("bti,kt->bki", along_dst, c_rows, precision=highest)
        slot_share = jnp.einsum("bki,abk->ai", inner_sum, core, precision=highest)
        slot_share = jnp.where(is_live, slot_share, jnp.zeros_like(slot_share))
        row_start = where_at[0].astype(jnp.int32)
        anchor = jnp.zeros((), jnp.int32)
        current = lax.dynamic_slice(running, (anchor, row_start, anchor), (rank_a, 1, BI))
        running = lax.dynamic_update_slice(running, current + slot_share[:, None, :], (anchor, row_start, anchor))
        return running, None

    running = jnp.zeros((rank_a, NSB, BI), jnp.float32)
    running, _ = lax.scan(per_block, running, (values, until, blocks, live_slots))
    return running.reshape(rank_a, NSB * BI)
```

```python
import functools

import jax
import jax.numpy as jnp
from jax import lax
from jax.experimental import pallas as pl
from jax.experimental.pallas import tpu as pltpu
from jax.sharding import PartitionSpec as P

BI = 128
BJ = 128
BT = 32
CHUNK = 16
GROUP = 8
MESH = pl.DeviceIdType.MESH
NN = ((1,), (0,))
NT = ((1,), (1,))


def dot(x, y, contract):
    return lax.dot_general(x, y, (contract, ((), ())), preferred_element_type=jnp.float32)


def split(x):
    high = x.astype(jnp.bfloat16)
    return high, (x - high.astype(jnp.float32)).astype(jnp.bfloat16)


def project_hours(core_ref, c_rows, first_ref):
    half = core_ref.shape[0] // 2
    rows = c_rows.shape[0]
    c_wide = jnp.concatenate([c_rows] * 3, axis=1)
    for p in range(0, half, 2):
        x = jnp.concatenate([core_ref[p], core_ref[p + half], core_ref[p + 1], core_ref[p + 1 + half]], axis=1)
        high = x.astype(jnp.bfloat16)
        rest = x - high.astype(jnp.float32)
        mid, low = split(rest)
        first = dot(c_wide, jnp.concatenate([high, mid, low], axis=0), NN)
        first_ref[pl.ds(p, rows, stride=half), :] = first[:, :128]
        first_ref[pl.ds(p + 1, rows, stride=half), :] = first[:, 128:]


def share_of(n, values_ref, until_ref, a, b, first_ref):
    rank_a = a.shape[0]
    half = rank_a // 2
    none = jnp.zeros_like(b)
    b_top = jnp.concatenate([b, none], axis=1)
    b_low = jnp.concatenate([none, b], axis=1)
    b_wide = jnp.concatenate([b_top, b_low, b_top, b_low], axis=0)
    a_cols = jnp.concatenate([a, a], axis=0).T.astype(jnp.bfloat16)
    until = until_ref[n].astype(jnp.bfloat16)
    total = jnp.zeros((2 * rank_a, BI), jnp.float32)
    for start in range(0, BT, CHUNK):
        f = first_ref[pl.ds(pl.multiple_of((n * BT + start) * half, CHUNK * half), CHUNK * half), :]
        second = dot(jnp.concatenate(split(f), axis=1), b_wide, NN)
        s_high, s_low = split(second)
        for group in range(0, CHUNK, GROUP):
            columns, parts = [], []
            for t in range(group, group + GROUP):
                rows = slice(t * half, (t + 1) * half)
                columns.append(jnp.concatenate(
                    [s_high[rows, :128], s_high[rows, 128:], s_low[rows, :128], s_low[rows, 128:]], axis=0))
            columns = jnp.concatenate(columns, axis=1)
            rebuilt = dot(a_cols, columns, NN).astype(jnp.bfloat16)
            for t in range(GROUP):
                hour = start + group + t
                guess = rebuilt[:, t * 128:(t + 1) * 128]
                parts.append(jnp.where(jnp.bfloat16(hour) < until, values_ref[n, hour], guess))
            total = total + dot(columns, jnp.concatenate(parts, axis=1), NT)
    return total[:rank_a] + total[rank_a:]


def step_kernel(n_src, n_dst, values_hbm, until_hbm, a_hbm, b_hbm, core_hbm, c_ref, blocks_ref, count_ref,
                share_out, ids_out, count_out,
                values, until, a_own, b_own, a_cut, b_cut, core, c_all, c_flat, ids_src, a_send, a_get, b_send, b_get, a_all, b_all,
                first, shares,
                in_sem, v_sem, c_send, c_recv, h_send, h_recv, i_send, i_recv, j_send, j_recv,
                k_send, k_recv, as_sem, ar_sem, bs_sem, br_sem, s_send, s_recv):
    src, dst = lax.axis_index("src"), lax.axis_index("dst")
    slots = values.shape[0]
    each_a, each_b = a_own.shape[0], b_own.shape[0]
    src_blocks, dst_blocks = a_own.shape[1] // BI, b_own.shape[1] // BJ

    loads = [
        pltpu.make_async_copy(a_hbm, a_own, in_sem.at[0]),
        pltpu.make_async_copy(b_hbm, b_own, in_sem.at[1]),
        pltpu.make_async_copy(core_hbm, core, in_sem.at[2]),
        pltpu.make_async_copy(until_hbm, until, in_sem.at[3]),
    ]
    for copy in loads:
        copy.start()
    for n in range(slots):
        pltpu.make_async_copy(values_hbm.at[n], values.at[n], v_sem.at[n]).start()

    def src_peer(step):
        return (lax.rem(src + step, n_src), dst)

    def dst_peer(step):
        return (src, lax.rem(dst + step, n_dst))

    barrier = pltpu.get_barrier_semaphore()
    for step in range(1, n_dst):
        pl.semaphore_signal(barrier, inc=1, device_id=dst_peer(step), device_id_type=MESH)
    for step in range(1, n_src):
        pl.semaphore_signal(barrier, inc=1, device_id=src_peer(step), device_id_type=MESH)

    def remote(source, target, send, recv, peer):
        return pltpu.make_async_remote_copy(
            src_ref=source, dst_ref=target, send_sem=send, recv_sem=recv, device_id=peer, device_id_type=MESH)

    hours_own, rank_c = c_ref.shape
    c_all[src, dst] = jnp.concatenate(
        [c_ref[...].astype(jnp.float32), jnp.zeros((hours_own, 128 - rank_c), jnp.float32)], axis=1)
    pl.semaphore_wait(barrier, n_dst - 1 + n_src - 1)

    hours, near, far = [], [], []
    for step in range(1, n_src):
        peer = src_peer(step)
        hours.append(remote(c_all.at[src, dst], c_all.at[src, dst], c_send.at[step - 1], c_recv.at[step - 1], peer))
        hours[-1].start()
        far.append(remote(blocks_ref, ids_src.at[src], i_send.at[step - 1], i_recv.at[step - 1], peer))
        far[-1].start()
    for step in range(1, n_dst):
        near.append(remote(blocks_ref, ids_out.at[dst], j_send.at[step - 1], j_recv.at[step - 1], dst_peer(step)))
        near[-1].start()
    counts = [pltpu.make_async_copy(count_ref, count_out.at[dst], in_sem.at[5])]
    for step in range(1, n_dst):
        counts.append(remote(count_ref, count_out.at[dst], k_send.at[step - 1], k_recv.at[step - 1], dst_peer(step)))
    own_ids = pltpu.make_async_copy(blocks_ref, ids_out.at[dst], in_sem.at[4])
    for copy in counts + [own_ids]:
        copy.start()
    for copy in loads[:2]:
        copy.wait()

    for s in range(src_blocks):
        a_cut[s] = a_own[:, s * BI:(s + 1) * BI].astype(jnp.float32)
    for d in range(dst_blocks):
        b_cut[d] = b_own[:, d * BJ:(d + 1) * BJ].astype(jnp.float32)

    def a_blocks(ids):
        blocks = [a_cut[lax.rem(ids[0, n], src_blocks)] for n in range(slots)]
        return jnp.concatenate(blocks, axis=0).astype(jnp.bfloat16)

    def b_blocks(ids):
        blocks = [b_cut[lax.rem(ids[1, n], dst_blocks)] for n in range(slots)]
        return jnp.concatenate(blocks, axis=0).astype(jnp.bfloat16)

    a_get[dst] = a_blocks(blocks_ref)
    b_get[src] = b_blocks(blocks_ref)

    for copy in hours:
        copy.wait()
    onward = []
    for step in range(1, n_dst):
        onward.append(remote(
            c_all.at[:, dst], c_all.at[:, dst], h_send.at[step - 1], h_recv.at[step - 1], dst_peer(step)))
        onward[-1].start()

    parts = []
    for step in range(1, n_src):
        far[step - 1].wait()
        back = lax.rem(src + n_src - step, n_src)
        b_send[step - 1] = b_blocks(ids_src.at[back])
        parts.append(remote(b_send.at[step - 1], b_get.at[src], bs_sem.at[step - 1], br_sem.at[step - 1], (back, dst)))
        parts[-1].start()
    for step in range(1, n_dst):
        near[step - 1].wait()
        back = lax.rem(dst + n_dst - step, n_dst)
        a_send[step - 1] = a_blocks(ids_out.at[back])
        parts.append(remote(a_send.at[step - 1], a_get.at[dst], as_sem.at[step - 1], ar_sem.at[step - 1], (src, back)))
        parts[-1].start()

    for copy in onward:
        copy.wait()
    c_flat[...] = c_all[...].reshape(c_flat.shape)
    c_rows = jnp.concatenate([c_flat[blocks_ref[2, n]] for n in range(slots)], axis=0)
    loads[2].wait()
    project_hours(core, c_rows[:, :rank_c].astype(jnp.bfloat16), first)

    for copy in parts + counts + [own_ids, loads[3]]:
        copy.wait()
    for p in range(n_src):
        part = b_get[p].astype(jnp.float32)
        for n in range(slots):
            b_all[n, p * each_b:(p + 1) * each_b, :] = part[n * each_b:(n + 1) * each_b]
    for q in range(n_dst):
        part = a_get[q].astype(jnp.float32)
        for n in range(slots):
            a_all[n, q * each_a:(q + 1) * each_a, :] = part[n * each_a:(n + 1) * each_a]

    def to_peer(n, step):
        peer = lax.rem(dst + step, n_dst)
        return remote(shares.at[peer, n], share_out.at[dst, n], s_send.at[n, step - 1], s_recv.at[n, step - 1], (src, peer))

    def one_slot(n, carry):
        pltpu.make_async_copy(values_hbm.at[n], values.at[n], v_sem.at[n]).wait()
        share = share_of(n, values, until, a_all[n], b_all[n].astype(jnp.bfloat16), first)
        for q in range(n_dst):
            shares[q, n] = share[q * each_a:(q + 1) * each_a]
        share_out[dst, n] = shares[dst, n]
        for step in range(1, n_dst):
            to_peer(n, step).start()
        return carry

    lax.fori_loop(0, slots, one_slot, 0)

    def finish(n, carry):
        for step in range(1, n_dst):
            to_peer(n, step).wait()
        return carry

    lax.fori_loop(0, slots, finish, 0)


def slot_shares(n_src, n_dst, values, until, blocks, count, a, b, c, core):
    slots = values.shape[0]
    rank_a, rank_c, rank_b = core.shape
    each_a, each_b = a.shape[0], b.shape[0]
    vmem = pl.BlockSpec(memory_space=pltpu.VMEM)
    smem = pl.BlockSpec(memory_space=pltpu.SMEM)
    hbm = pl.BlockSpec(memory_space=pl.ANY)
    dma = pltpu.SemaphoreType.DMA
    far, near = dma((n_src - 1,)), dma((n_dst - 1,))
    return pl.pallas_call(
        functools.partial(step_kernel, n_src, n_dst),
        out_shape=(
            jax.ShapeDtypeStruct((n_dst, slots, each_a, BI), jnp.float32),
            jax.ShapeDtypeStruct((n_dst,) + blocks.shape, jnp.int32),
            jax.ShapeDtypeStruct((n_dst,) + count.shape, jnp.int32),
        ),
        in_specs=[hbm] * 5 + [vmem, smem, smem],
        out_specs=(vmem, smem, smem),
        scratch_shapes=[
            pltpu.VMEM(values.shape, values.dtype),
            pltpu.VMEM(until.shape, until.dtype),
            pltpu.VMEM(a.shape, a.dtype),
            pltpu.VMEM(b.shape, b.dtype),
            pltpu.VMEM((a.shape[1] // BI, each_a, BI), jnp.float32),
            pltpu.VMEM((b.shape[1] // BJ, each_b, BJ), jnp.float32),
            pltpu.VMEM(core.shape, core.dtype),
            pltpu.VMEM((n_src, n_dst, c.shape[0], 128), jnp.float32),
            pltpu.VMEM((n_src * n_dst * c.shape[0] // BT, BT, 128), jnp.float32),
            pltpu.SMEM((n_src,) + blocks.shape, jnp.int32),
            pltpu.VMEM((n_dst - 1, slots * each_a, BI), a.dtype),
            pltpu.VMEM((n_dst, slots * each_a, BI), a.dtype),
            pltpu.VMEM((n_src - 1, slots * each_b, BJ), b.dtype),
            pltpu.VMEM((n_src, slots * each_b, BJ), b.dtype),
            pltpu.VMEM((slots, rank_a, BI), jnp.float32),
            pltpu.VMEM((slots, rank_b, BJ), jnp.float32),
            pltpu.VMEM((slots * BT * rank_a // 2, 128), jnp.float32),
            pltpu.VMEM((n_dst, slots, each_a, BI), jnp.float32),
            dma((6,)), dma((slots,)), far, far, near, near, far, far, near, near, near, near,
            near, near, far, far, dma((slots, n_dst - 1)), dma((slots, n_dst - 1)),
        ],
        compiler_params=pltpu.CompilerParams(
            collective_id=0, has_side_effects=True, vmem_limit_bytes=48 * 2 ** 20),
        name="slot_shares",
    )(values, until, a, b, core, c, blocks, count)


def sum_kernel(ids_ref, count_ref, share_ref, out_ref):
    out_ref[...] = jnp.zeros_like(out_ref)
    blocks = out_ref.shape[1] // BI
    for q in range(share_ref.shape[0]):
        for n in range(share_ref.shape[1]):
            @pl.when(n < count_ref[q, 0])
            def _():
                column = pl.ds(pl.multiple_of(lax.rem(ids_ref[q, 0, n], blocks) * BI, BI), BI)
                out_ref[:, column] += share_ref[q, n]


def sum_shares(ids, counts, shares, columns):
    vmem = pl.BlockSpec(memory_space=pltpu.VMEM)
    smem = pl.BlockSpec(memory_space=pltpu.SMEM)
    return pl.pallas_call(
        sum_kernel,
        out_shape=jax.ShapeDtypeStruct((shares.shape[2], columns), jnp.float32),
        in_specs=[smem, smem, vmem],
        out_specs=vmem,
        name="sum_shares",
    )(ids, counts, shares)


def on_device(n_src, n_dst, values, until, blocks, count, a_factor, b_factor, c_factor, core):
    shares, ids, counts = slot_shares(
        n_src, n_dst, values, until, blocks.T, count, a_factor, b_factor, c_factor.T, core.transpose(0, 2, 1))
    return sum_shares(ids, counts, shares, a_factor.shape[1])


def solution(mesh):
    return jax.shard_map(
        functools.partial(on_device, mesh.shape["src"], mesh.shape["dst"]),
        mesh=mesh,
        in_specs=(
            P(("src", "dst"), None, None, None),
            P(("src", "dst"), None, None),
            P(("src", "dst"), None),
            P(("src", "dst")),
            P("dst", "src"),
            P("src", "dst"),
            P(None, ("src", "dst")),
            P(),
        ),
        out_specs=P("dst", "src"),
        check_vma=False,
    )
```

```python
import functools

import jax
import jax.numpy as jnp
from jax import lax
from jax.experimental import pallas as pl
from jax.experimental.pallas import tpu as pltpu
from jax.sharding import PartitionSpec as P

BI = 128
BJ = 128
BT = 32
CHUNK = 16
GROUP = 8
MESH = pl.DeviceIdType.MESH
NN = ((1,), (0,))
NT = ((1,), (1,))


def dot(x, y, contract):
    return lax.dot_general(x, y, (contract, ((), ())), preferred_element_type=jnp.float32)


def split(x):
    high = x.astype(jnp.bfloat16)
    return high, (x - high.astype(jnp.float32)).astype(jnp.bfloat16)


def project_hours(core_ref, c_rows, first_ref):
    half = core_ref.shape[0] // 2
    rows = c_rows.shape[0]
    c_wide = jnp.concatenate([c_rows] * 3, axis=1)
    for p in range(0, half, 2):
        x = jnp.concatenate([core_ref[p], core_ref[p + half], core_ref[p + 1], core_ref[p + 1 + half]], axis=1)
        high = x.astype(jnp.bfloat16)
        rest = x - high.astype(jnp.float32)
        mid, low = split(rest)
        first = dot(c_wide, jnp.concatenate([high, mid, low], axis=0), NN)
        first_ref[pl.ds(p, rows, stride=half), :] = first[:, :128]
        first_ref[pl.ds(p + 1, rows, stride=half), :] = first[:, 128:]


def share_of(n, values_ref, until_ref, a, b, first_ref):
    rank_a = a.shape[0]
    half = rank_a // 2
    none = jnp.zeros_like(b)
    b_top = jnp.concatenate([b, none], axis=1)
    b_low = jnp.concatenate([none, b], axis=1)
    b_wide = jnp.concatenate([b_top, b_low, b_top, b_low], axis=0)
    a_cols = jnp.concatenate([a, a], axis=0).T.astype(jnp.bfloat16)
    until = until_ref[n].astype(jnp.bfloat16)
    total = jnp.zeros((2 * rank_a, BI), jnp.float32)
    for start in range(0, BT, CHUNK):
        f = first_ref[pl.ds(pl.multiple_of((n * BT + start) * half, CHUNK * half), CHUNK * half), :]
        second = dot(jnp.concatenate(split(f), axis=1), b_wide, NN)
        s_high, s_low = split(second)
        for group in range(0, CHUNK, GROUP):
            columns, parts = [], []
            for t in range(group, group + GROUP):
                rows = slice(t * half, (t + 1) * half)
                columns.append(jnp.concatenate(
                    [s_high[rows, :128], s_high[rows, 128:], s_low[rows, :128], s_low[rows, 128:]], axis=0))
            columns = jnp.concatenate(columns, axis=1)
            rebuilt = dot(a_cols, columns, NN).astype(jnp.bfloat16)
            for t in range(GROUP):
                hour = start + group + t
                guess = rebuilt[:, t * 128:(t + 1) * 128]
                parts.append(jnp.where(jnp.bfloat16(hour) < until, values_ref[n, hour], guess))
            total = total + dot(columns, jnp.concatenate(parts, axis=1), NT)
    return total[:rank_a] + total[rank_a:]


def step_kernel(n_src, n_dst, values_hbm, until_hbm, a_hbm, b_hbm, core_hbm, c_hbm, blocks_hbm, count_hbm,
                share_out, ids_out, count_out,
                c_ref, blocks_ref, count_ref, values, until, a_own, b_own, a_cut, b_cut, core, c_all, c_flat, ids_src, a_send, a_get, b_send, b_get, a_all, b_all,
                first, shares,
                in_sem, v_sem, c_send, c_recv, h_send, h_recv, i_send, i_recv, j_send, j_recv,
                k_send, k_recv, as_sem, ar_sem, bs_sem, br_sem, s_send, s_recv):
    src, dst = lax.axis_index("src"), lax.axis_index("dst")
    slots = values.shape[0]
    each_a, each_b = a_own.shape[0], b_own.shape[0]
    src_blocks, dst_blocks = a_own.shape[1] // BI, b_own.shape[1] // BJ

    small = [
        pltpu.make_async_copy(blocks_hbm, blocks_ref, in_sem.at[6]),
        pltpu.make_async_copy(c_hbm, c_ref, in_sem.at[7]),
        pltpu.make_async_copy(count_hbm, count_ref, in_sem.at[8]),
    ]
    loads = [
        pltpu.make_async_copy(a_hbm, a_own, in_sem.at[0]),
        pltpu.make_async_copy(b_hbm, b_own, in_sem.at[1]),
        pltpu.make_async_copy(core_hbm, core, in_sem.at[2]),
        pltpu.make_async_copy(until_hbm, until, in_sem.at[3]),
    ]
    for copy in small + loads:
        copy.start()
    for n in range(slots):
        pltpu.make_async_copy(values_hbm.at[n], values.at[n], v_sem.at[n]).start()

    def src_peer(step):
        return (lax.rem(src + step, n_src), dst)

    def dst_peer(step):
        return (src, lax.rem(dst + step, n_dst))

    barrier = pltpu.get_barrier_semaphore()
    for step in range(1, n_dst):
        pl.semaphore_signal(barrier, inc=1, device_id=dst_peer(step), device_id_type=MESH)
    for step in range(1, n_src):
        pl.semaphore_signal(barrier, inc=1, device_id=src_peer(step), device_id_type=MESH)

    def remote(source, target, send, recv, peer):
        return pltpu.make_async_remote_copy(
            src_ref=source, dst_ref=target, send_sem=send, recv_sem=recv, device_id=peer, device_id_type=MESH)

    for copy in small:
        copy.wait()
    hours_own, rank_c = c_ref.shape
    c_all[src, dst] = jnp.concatenate(
        [c_ref[...].astype(jnp.float32), jnp.zeros((hours_own, 128 - rank_c), jnp.float32)], axis=1)
    pl.semaphore_wait(barrier, n_dst - 1 + n_src - 1)

    hours, near, far = [], [], []
    for step in range(1, n_src):
        peer = src_peer(step)
        hours.append(remote(c_all.at[src, dst], c_all.at[src, dst], c_send.at[step - 1], c_recv.at[step - 1], peer))
        hours[-1].start()
        far.append(remote(blocks_ref, ids_src.at[src], i_send.at[step - 1], i_recv.at[step - 1], peer))
        far[-1].start()
    for step in range(1, n_dst):
        near.append(remote(blocks_ref, ids_out.at[dst], j_send.at[step - 1], j_recv.at[step - 1], dst_peer(step)))
        near[-1].start()
    counts = [pltpu.make_async_copy(count_ref, count_out.at[dst], in_sem.at[5])]
    for step in range(1, n_dst):
        counts.append(remote(count_ref, count_out.at[dst], k_send.at[step - 1], k_recv.at[step - 1], dst_peer(step)))
    own_ids = pltpu.make_async_copy(blocks_ref, ids_out.at[dst], in_sem.at[4])
    for copy in counts + [own_ids]:
        copy.start()
    for copy in loads[:2]:
        copy.wait()

    for s in range(src_blocks):
        a_cut[s] = a_own[:, s * BI:(s + 1) * BI].astype(jnp.float32)
    for d in range(dst_blocks):
        b_cut[d] = b_own[:, d * BJ:(d + 1) * BJ].astype(jnp.float32)

    def a_blocks(ids):
        blocks = [a_cut[lax.rem(ids[0, n], src_blocks)] for n in range(slots)]
        return jnp.concatenate(blocks, axis=0).astype(jnp.bfloat16)

    def b_blocks(ids):
        blocks = [b_cut[lax.rem(ids[1, n], dst_blocks)] for n in range(slots)]
        return jnp.concatenate(blocks, axis=0).astype(jnp.bfloat16)

    a_get[dst] = a_blocks(blocks_ref)
    b_get[src] = b_blocks(blocks_ref)

    for copy in hours:
        copy.wait()
    onward = []
    for step in range(1, n_dst):
        onward.append(remote(
            c_all.at[:, dst], c_all.at[:, dst], h_send.at[step - 1], h_recv.at[step - 1], dst_peer(step)))
        onward[-1].start()

    parts = []
    for step in range(1, n_src):
        far[step - 1].wait()
        back = lax.rem(src + n_src - step, n_src)
        b_send[step - 1] = b_blocks(ids_src.at[back])
        parts.append(remote(b_send.at[step - 1], b_get.at[src], bs_sem.at[step - 1], br_sem.at[step - 1], (back, dst)))
        parts[-1].start()
    for step in range(1, n_dst):
        near[step - 1].wait()
        back = lax.rem(dst + n_dst - step, n_dst)
        a_send[step - 1] = a_blocks(ids_out.at[back])
        parts.append(remote(a_send.at[step - 1], a_get.at[dst], as_sem.at[step - 1], ar_sem.at[step - 1], (src, back)))
        parts[-1].start()

    for copy in onward:
        copy.wait()
    c_flat[...] = c_all[...].reshape(c_flat.shape)
    c_rows = jnp.concatenate([c_flat[blocks_ref[2, n]] for n in range(slots)], axis=0)
    loads[2].wait()
    project_hours(core, c_rows[:, :rank_c].astype(jnp.bfloat16), first)

    for copy in parts + counts + [own_ids, loads[3]]:
        copy.wait()
    for p in range(n_src):
        part = b_get[p].astype(jnp.float32)
        for n in range(slots):
            b_all[n, p * each_b:(p + 1) * each_b, :] = part[n * each_b:(n + 1) * each_b]
    for q in range(n_dst):
        part = a_get[q].astype(jnp.float32)
        for n in range(slots):
            a_all[n, q * each_a:(q + 1) * each_a, :] = part[n * each_a:(n + 1) * each_a]

    def to_peer(n, step):
        peer = lax.rem(dst + step, n_dst)
        return remote(shares.at[peer, n], share_out.at[dst, n], s_send.at[n, step - 1], s_recv.at[n, step - 1], (src, peer))

    def one_slot(n, carry):
        pltpu.make_async_copy(values_hbm.at[n], values.at[n], v_sem.at[n]).wait()
        share = share_of(n, values, until, a_all[n], b_all[n].astype(jnp.bfloat16), first)
        for q in range(n_dst):
            shares[q, n] = share[q * each_a:(q + 1) * each_a]
        share_out[dst, n] = shares[dst, n]
        for step in range(1, n_dst):
            to_peer(n, step).start()
        return carry

    lax.fori_loop(0, slots, one_slot, 0)

    def finish(n, carry):
        for step in range(1, n_dst):
            to_peer(n, step).wait()
        return carry

    lax.fori_loop(0, slots, finish, 0)


def slot_shares(n_src, n_dst, values, until, blocks, count, a, b, c, core):
    slots = values.shape[0]
    rank_a, rank_c, rank_b = core.shape
    each_a, each_b = a.shape[0], b.shape[0]
    vmem = pl.BlockSpec(memory_space=pltpu.VMEM)
    smem = pl.BlockSpec(memory_space=pltpu.SMEM)
    hbm = pl.BlockSpec(memory_space=pltpu.HBM)
    dma = pltpu.SemaphoreType.DMA
    far, near = dma((n_src - 1,)), dma((n_dst - 1,))
    return pl.pallas_call(
        functools.partial(step_kernel, n_src, n_dst),
        out_shape=(
            jax.ShapeDtypeStruct((n_dst, slots, each_a, BI), jnp.float32),
            jax.ShapeDtypeStruct((n_dst,) + blocks.shape, jnp.int32),
            jax.ShapeDtypeStruct((n_dst,) + count.shape, jnp.int32),
        ),
        in_specs=[hbm] * 8,
        out_specs=(vmem, smem, smem),
        scratch_shapes=[
            pltpu.VMEM(c.shape, c.dtype),
            pltpu.SMEM(blocks.shape, blocks.dtype),
            pltpu.SMEM(count.shape, count.dtype),
            pltpu.VMEM(values.shape, values.dtype),
            pltpu.VMEM(until.shape, until.dtype),
            pltpu.VMEM(a.shape, a.dtype),
            pltpu.VMEM(b.shape, b.dtype),
            pltpu.VMEM((a.shape[1] // BI, each_a, BI), jnp.float32),
            pltpu.VMEM((b.shape[1] // BJ, each_b, BJ), jnp.float32),
            pltpu.VMEM(core.shape, core.dtype),
            pltpu.VMEM((n_src, n_dst, c.shape[0], 128), jnp.float32),
            pltpu.VMEM((n_src * n_dst * c.shape[0] // BT, BT, 128), jnp.float32),
            pltpu.SMEM((n_src,) + blocks.shape, jnp.int32),
            pltpu.VMEM((n_dst - 1, slots * each_a, BI), a.dtype),
            pltpu.VMEM((n_dst, slots * each_a, BI), a.dtype),
            pltpu.VMEM((n_src - 1, slots * each_b, BJ), b.dtype),
            pltpu.VMEM((n_src, slots * each_b, BJ), b.dtype),
            pltpu.VMEM((slots, rank_a, BI), jnp.float32),
            pltpu.VMEM((slots, rank_b, BJ), jnp.float32),
            pltpu.VMEM((slots * BT * rank_a // 2, 128), jnp.float32),
            pltpu.VMEM((n_dst, slots, each_a, BI), jnp.float32),
            dma((9,)), dma((slots,)), far, far, near, near, far, far, near, near, near, near,
            near, near, far, far, dma((slots, n_dst - 1)), dma((slots, n_dst - 1)),
        ],
        compiler_params=pltpu.CompilerParams(
            collective_id=0, has_side_effects=True, vmem_limit_bytes=64 * 2 ** 20),
        name="slot_shares",
    )(values, until, a, b, core, c, blocks, count)


def sum_kernel(ids_ref, count_ref, share_ref, out_ref):
    out_ref[...] = jnp.zeros_like(out_ref)
    blocks = out_ref.shape[1] // BI
    for q in range(share_ref.shape[0]):
        for n in range(share_ref.shape[1]):
            @pl.when(n < count_ref[q, 0])
            def _():
                column = pl.ds(pl.multiple_of(lax.rem(ids_ref[q, 0, n], blocks) * BI, BI), BI)
                out_ref[:, column] += share_ref[q, n]


def sum_shares(ids, counts, shares, columns):
    vmem = pl.BlockSpec(memory_space=pltpu.VMEM)
    smem = pl.BlockSpec(memory_space=pltpu.SMEM)
    return pl.pallas_call(
        sum_kernel,
        out_shape=jax.ShapeDtypeStruct((shares.shape[2], columns), jnp.float32),
        in_specs=[smem, smem, vmem],
        out_specs=vmem,
        compiler_params=pltpu.CompilerParams(vmem_limit_bytes=64 * 2 ** 20),
        name="sum_shares",
    )(ids, counts, shares)


def on_device(n_src, n_dst, values, until, blocks, count, a_factor, b_factor, c_factor, core):
    shares, ids, counts = slot_shares(
        n_src, n_dst, values, until, blocks.T, count, a_factor, b_factor, c_factor.T, core.transpose(0, 2, 1))
    return sum_shares(ids, counts, shares, a_factor.shape[1])


def solution(mesh):
    return jax.shard_map(
        functools.partial(on_device, mesh.shape["src"], mesh.shape["dst"]),
        mesh=mesh,
        in_specs=(
            P(("src", "dst"), None, None, None),
            P(("src", "dst"), None, None),
            P(("src", "dst"), None),
            P(("src", "dst")),
            P("dst", "src"),
            P("src", "dst"),
            P(None, ("src", "dst")),
            P(),
        ),
        out_specs=P("dst", "src"),
        check_vma=False,
    )
```

```python
import functools
import math

import jax
import jax.numpy as jnp
from jax import lax
from jax.experimental import pallas as pl
from jax.experimental.pallas import tpu as pltpu
from jax.sharding import PartitionSpec as P

BI = 128
BJ = 128
BT = 32
CHUNK = 8
AHEAD = 2
TOGETHER = 4
MESH = pl.DeviceIdType.MESH
NN = ((1,), (0,))
NT = ((1,), (1,))


def dot(x, y, contract):
    return lax.dot_general(x, y, (contract, ((), ())), preferred_element_type=jnp.float32)


def split(x):
    high = x.astype(jnp.bfloat16)
    return high, (x - high.astype(jnp.float32)).astype(jnp.bfloat16)


def project_hours(core_ref, c_rows, first_ref):
    half = core_ref.shape[0] // 2
    rows = c_rows.shape[0]
    c_wide = jnp.concatenate([c_rows] * 3, axis=1)
    for p in range(0, half, 2):
        x = jnp.concatenate([core_ref[p], core_ref[p + half], core_ref[p + 1], core_ref[p + 1 + half]], axis=1)
        high = x.astype(jnp.bfloat16)
        rest = x - high.astype(jnp.float32)
        mid, low = split(rest)
        first = dot(c_wide, jnp.concatenate([high, mid, low], axis=0), NN)
        first_ref[pl.ds(p, rows, stride=half), :] = first[:, :128]
        first_ref[pl.ds(p + 1, rows, stride=half), :] = first[:, 128:]


def shares_of(slots, values_ref, until_ref, a_all, b_all, first_ref):
    half = a_all.shape[1] // 2
    sides = {}

    def begin(n):
        a, b = a_all[n], b_all[n].astype(jnp.bfloat16)
        none = jnp.zeros_like(b)
        b_top = jnp.concatenate([b, none], axis=1)
        b_low = jnp.concatenate([none, b], axis=1)
        b_wide = jnp.concatenate([b_top, b_low, b_top, b_low], axis=0)
        a_cols = jnp.concatenate([a, a], axis=0).T.astype(jnp.bfloat16)
        return b_wide, a_cols, until_ref[n].astype(jnp.bfloat16)

    def project(n, start, b_wide):
        rows = pl.ds(pl.multiple_of((n * BT + start) * half, CHUNK * half), CHUNK * half)
        second = dot(jnp.concatenate(split(first_ref[rows, :]), axis=1), b_wide, NN)
        high, low = split(second)
        columns = []
        for t in range(CHUNK):
            rows = slice(t * half, (t + 1) * half)
            columns.append(jnp.concatenate(
                [high[rows, :128], high[rows, 128:], low[rows, :128], low[rows, 128:]], axis=0))
        return jnp.concatenate(columns, axis=1)

    def impute(n, start, columns, a_cols, until):
        rebuilt = dot(a_cols, columns, NN).astype(jnp.bfloat16)
        return jnp.concatenate([
            jnp.where(jnp.bfloat16(start + t) < until, values_ref[n, start + t], rebuilt[:, t * 128:(t + 1) * 128])
            for t in range(CHUNK)], axis=1)

    turns = [(u, start) for start in range(0, BT, CHUNK) for u in range(len(slots))]
    columns, imputed, totals = {}, {}, {}
    for k in range(len(turns) + AHEAD + 1):
        if k < len(turns):
            u, start = turns[k]
            if u not in sides:
                sides[u] = begin(slots[u])
            columns[k] = project(slots[u], start, sides[u][0])
        j = k - AHEAD
        if 0 <= j < len(turns):
            u, start = turns[j]
            imputed[j] = impute(slots[u], start, columns[j], *sides[u][1:])
        j = k - AHEAD - 1
        if j >= 0:
            u, _ = turns[j]
            term = dot(columns.pop(j), imputed.pop(j), NT)
            totals[u] = totals[u] + term if u in totals else term
    return [totals[u][:2 * half] + totals[u][2 * half:] for u in range(len(slots))]


def step_kernel(n_src, n_dst, values_hbm, until_hbm, a_hbm, b_hbm, core_hbm, c_hbm, blocks_hbm, count_hbm,
                share_out, ids_out, count_out,
                c_ref, blocks_ref, count_ref, values, until, a_own, b_own, a_cut, b_cut, core, c_all, c_flat, ids_src, a_send, a_get, b_send, b_get, a_all, b_all,
                first, shares,
                in_sem, v_sem, c_send, c_recv, h_send, h_recv, i_send, i_recv, j_send, j_recv,
                k_send, k_recv, as_sem, ar_sem, bs_sem, br_sem, s_send, s_recv):
    src, dst = lax.axis_index("src"), lax.axis_index("dst")
    slots = values.shape[0]
    each_a, each_b = a_own.shape[0], b_own.shape[0]
    src_blocks, dst_blocks = a_own.shape[1] // BI, b_own.shape[1] // BJ

    small = [
        pltpu.make_async_copy(blocks_hbm, blocks_ref, in_sem.at[6]),
        pltpu.make_async_copy(c_hbm, c_ref, in_sem.at[7]),
        pltpu.make_async_copy(count_hbm, count_ref, in_sem.at[8]),
    ]
    loads = [
        pltpu.make_async_copy(a_hbm, a_own, in_sem.at[0]),
        pltpu.make_async_copy(b_hbm, b_own, in_sem.at[1]),
        pltpu.make_async_copy(core_hbm, core, in_sem.at[2]),
        pltpu.make_async_copy(until_hbm, until, in_sem.at[3]),
    ]
    for copy in small + loads:
        copy.start()
    for n in range(slots):
        pltpu.make_async_copy(values_hbm.at[n], values.at[n], v_sem.at[n]).start()

    def src_peer(step):
        return (lax.rem(src + step, n_src), dst)

    def dst_peer(step):
        return (src, lax.rem(dst + step, n_dst))

    barrier = pltpu.get_barrier_semaphore()
    for step in range(1, n_dst):
        pl.semaphore_signal(barrier, inc=1, device_id=dst_peer(step), device_id_type=MESH)
    for step in range(1, n_src):
        pl.semaphore_signal(barrier, inc=1, device_id=src_peer(step), device_id_type=MESH)

    def remote(source, target, send, recv, peer):
        return pltpu.make_async_remote_copy(
            src_ref=source, dst_ref=target, send_sem=send, recv_sem=recv, device_id=peer, device_id_type=MESH)

    for copy in small:
        copy.wait()
    hours_own, rank_c = c_ref.shape
    c_all[src, dst] = jnp.concatenate(
        [c_ref[...].astype(jnp.float32), jnp.zeros((hours_own, 128 - rank_c), jnp.float32)], axis=1)
    pl.semaphore_wait(barrier, n_dst - 1 + n_src - 1)

    hours, near, far = [], [], []
    for step in range(1, n_src):
        peer = src_peer(step)
        hours.append(remote(c_all.at[src, dst], c_all.at[src, dst], c_send.at[step - 1], c_recv.at[step - 1], peer))
        hours[-1].start()
        far.append(remote(blocks_ref, ids_src.at[src], i_send.at[step - 1], i_recv.at[step - 1], peer))
        far[-1].start()
    for step in range(1, n_dst):
        near.append(remote(blocks_ref, ids_out.at[dst], j_send.at[step - 1], j_recv.at[step - 1], dst_peer(step)))
        near[-1].start()
    counts = [pltpu.make_async_copy(count_ref, count_out.at[dst], in_sem.at[5])]
    for step in range(1, n_dst):
        counts.append(remote(count_ref, count_out.at[dst], k_send.at[step - 1], k_recv.at[step - 1], dst_peer(step)))
    own_ids = pltpu.make_async_copy(blocks_ref, ids_out.at[dst], in_sem.at[4])
    for copy in counts + [own_ids]:
        copy.start()
    for copy in loads[:2]:
        copy.wait()

    for s in range(src_blocks):
        a_cut[s] = a_own[:, s * BI:(s + 1) * BI].astype(jnp.float32)
    for d in range(dst_blocks):
        b_cut[d] = b_own[:, d * BJ:(d + 1) * BJ].astype(jnp.float32)

    def a_blocks(ids):
        blocks = [a_cut[lax.rem(ids[0, n], src_blocks)] for n in range(slots)]
        return jnp.concatenate(blocks, axis=0).astype(jnp.bfloat16)

    def b_blocks(ids):
        blocks = [b_cut[lax.rem(ids[1, n], dst_blocks)] for n in range(slots)]
        return jnp.concatenate(blocks, axis=0).astype(jnp.bfloat16)

    a_get[dst] = a_blocks(blocks_ref)
    b_get[src] = b_blocks(blocks_ref)

    for copy in hours:
        copy.wait()
    onward = []
    for step in range(1, n_dst):
        onward.append(remote(
            c_all.at[:, dst], c_all.at[:, dst], h_send.at[step - 1], h_recv.at[step - 1], dst_peer(step)))
        onward[-1].start()

    parts = []
    for step in range(1, n_src):
        far[step - 1].wait()
        back = lax.rem(src + n_src - step, n_src)
        b_send[step - 1] = b_blocks(ids_src.at[back])
        parts.append(remote(b_send.at[step - 1], b_get.at[src], bs_sem.at[step - 1], br_sem.at[step - 1], (back, dst)))
        parts[-1].start()
    for step in range(1, n_dst):
        near[step - 1].wait()
        back = lax.rem(dst + n_dst - step, n_dst)
        a_send[step - 1] = a_blocks(ids_out.at[back])
        parts.append(remote(a_send.at[step - 1], a_get.at[dst], as_sem.at[step - 1], ar_sem.at[step - 1], (src, back)))
        parts[-1].start()

    for copy in onward:
        copy.wait()
    c_flat[...] = c_all[...].reshape(c_flat.shape)
    c_rows = jnp.concatenate([c_flat[blocks_ref[2, n]] for n in range(slots)], axis=0)
    loads[2].wait()
    project_hours(core, c_rows[:, :rank_c].astype(jnp.bfloat16), first)

    for copy in parts + counts + [own_ids, loads[3]]:
        copy.wait()
    for p in range(n_src):
        part = b_get[p].astype(jnp.float32)
        for n in range(slots):
            b_all[n, p * each_b:(p + 1) * each_b, :] = part[n * each_b:(n + 1) * each_b]
    for q in range(n_dst):
        part = a_get[q].astype(jnp.float32)
        for n in range(slots):
            a_all[n, q * each_a:(q + 1) * each_a, :] = part[n * each_a:(n + 1) * each_a]

    together = math.gcd(slots, TOGETHER)

    def to_peer(turn, step):
        peer = lax.rem(dst + step, n_dst)
        part = pl.ds(turn * together, together)
        return remote(shares.at[peer, part], share_out.at[dst, part],
                      s_send.at[turn, step - 1], s_recv.at[turn, step - 1], (src, peer))

    def some_slots(turn, carry):
        ns = [turn * together + u for u in range(together)]
        for n in ns:
            pltpu.make_async_copy(values_hbm.at[n], values.at[n], v_sem.at[n]).wait()
        for n, share in zip(ns, shares_of(ns, values, until, a_all, b_all, first)):
            for q in range(n_dst):
                shares[q, n] = share[q * each_a:(q + 1) * each_a]
            share_out[dst, n] = shares[dst, n]
        for step in range(1, n_dst):
            to_peer(turn, step).start()
        return carry

    lax.fori_loop(0, slots // together, some_slots, 0)
    for turn in range(slots // together):
        for step in range(1, n_dst):
            to_peer(turn, step).wait()


def slot_shares(n_src, n_dst, values, until, blocks, count, a, b, c, core):
    slots = values.shape[0]
    rank_a, rank_c, rank_b = core.shape
    each_a, each_b = a.shape[0], b.shape[0]
    vmem = pl.BlockSpec(memory_space=pltpu.VMEM)
    smem = pl.BlockSpec(memory_space=pltpu.SMEM)
    hbm = pl.BlockSpec(memory_space=pltpu.HBM)
    dma = pltpu.SemaphoreType.DMA
    far, near = dma((n_src - 1,)), dma((n_dst - 1,))
    return pl.pallas_call(
        functools.partial(step_kernel, n_src, n_dst),
        out_shape=(
            jax.ShapeDtypeStruct((n_dst, slots, each_a, BI), jnp.float32),
            jax.ShapeDtypeStruct((n_dst,) + blocks.shape, jnp.int32),
            jax.ShapeDtypeStruct((n_dst,) + count.shape, jnp.int32),
        ),
        in_specs=[hbm] * 8,
        out_specs=(vmem, smem, smem),
        scratch_shapes=[
            pltpu.VMEM(c.shape, c.dtype),
            pltpu.SMEM(blocks.shape, blocks.dtype),
            pltpu.SMEM(count.shape, count.dtype),
            pltpu.VMEM(values.shape, values.dtype),
            pltpu.VMEM(until.shape, until.dtype),
            pltpu.VMEM(a.shape, a.dtype),
            pltpu.VMEM(b.shape, b.dtype),
            pltpu.VMEM((a.shape[1] // BI, each_a, BI), jnp.float32),
            pltpu.VMEM((b.shape[1] // BJ, each_b, BJ), jnp.float32),
            pltpu.VMEM(core.shape, core.dtype),
            pltpu.VMEM((n_src, n_dst, c.shape[0], 128), jnp.float32),
            pltpu.VMEM((n_src * n_dst * c.shape[0] // BT, BT, 128), jnp.float32),
            pltpu.SMEM((n_src,) + blocks.shape, jnp.int32),
            pltpu.VMEM((n_dst - 1, slots * each_a, BI), a.dtype),
            pltpu.VMEM((n_dst, slots * each_a, BI), a.dtype),
            pltpu.VMEM((n_src - 1, slots * each_b, BJ), b.dtype),
            pltpu.VMEM((n_src, slots * each_b, BJ), b.dtype),
            pltpu.VMEM((slots, rank_a, BI), jnp.float32),
            pltpu.VMEM((slots, rank_b, BJ), jnp.float32),
            pltpu.VMEM((slots * BT * rank_a // 2, 128), jnp.float32),
            pltpu.VMEM((n_dst, slots, each_a, BI), jnp.float32),
            dma((9,)), dma((slots,)), far, far, near, near, far, far, near, near, near, near,
            near, near, far, far, dma((slots, n_dst - 1)), dma((slots, n_dst - 1)),
        ],
        compiler_params=pltpu.CompilerParams(
            collective_id=0, has_side_effects=True, vmem_limit_bytes=64 * 2 ** 20),
        name="slot_shares",
    )(values, until, a, b, core, c, blocks, count)


def sum_kernel(ids_ref, count_ref, share_ref, out_ref):
    out_ref[...] = jnp.zeros_like(out_ref)
    blocks = out_ref.shape[1] // BI
    for q in range(share_ref.shape[0]):
        for n in range(share_ref.shape[1]):
            @pl.when(n < count_ref[q, 0])
            def _():
                column = pl.ds(pl.multiple_of(lax.rem(ids_ref[q, 0, n], blocks) * BI, BI), BI)
                out_ref[:, column] += share_ref[q, n]


def sum_shares(ids, counts, shares, columns):
    vmem = pl.BlockSpec(memory_space=pltpu.VMEM)
    smem = pl.BlockSpec(memory_space=pltpu.SMEM)
    return pl.pallas_call(
        sum_kernel,
        out_shape=jax.ShapeDtypeStruct((shares.shape[2], columns), jnp.float32),
        in_specs=[smem, smem, vmem],
        out_specs=vmem,
        compiler_params=pltpu.CompilerParams(vmem_limit_bytes=64 * 2 ** 20),
        name="sum_shares",
    )(ids, counts, shares)


def on_device(n_src, n_dst, values, until, blocks, count, a_factor, b_factor, c_factor, core):
    shares, ids, counts = slot_shares(
        n_src, n_dst, values, until, blocks.T, count, a_factor, b_factor, c_factor.T, core.transpose(0, 2, 1))
    return sum_shares(ids, counts, shares, a_factor.shape[1])


def solution(mesh):
    return jax.shard_map(
        functools.partial(on_device, mesh.shape["src"], mesh.shape["dst"]),
        mesh=mesh,
        in_specs=(
            P(("src", "dst"), None, None, None),
            P(("src", "dst"), None, None),
            P(("src", "dst"), None),
            P(("src", "dst")),
            P("dst", "src"),
            P("src", "dst"),
            P(None, ("src", "dst")),
            P(),
        ),
        out_specs=P("dst", "src"),
        check_vma=False,
    )
```

```python
import functools
import math

import jax
import jax.numpy as jnp
from jax import lax
from jax.experimental import pallas as pl
from jax.experimental.pallas import tpu as pltpu
from jax.sharding import PartitionSpec as P

BI = 128
BJ = 128
BT = 32
CHUNK = 8
AHEAD = 2
TOGETHER = 4
MESH = pl.DeviceIdType.MESH
NN = ((1,), (0,))
NT = ((1,), (1,))


def dot(x, y, contract):
    return lax.dot_general(x, y, (contract, ((), ())), preferred_element_type=jnp.float32)


def split(x):
    high = x.astype(jnp.bfloat16)
    return high, (x - high.astype(jnp.float32)).astype(jnp.bfloat16)


def project_hours(core_ref, c_rows, first_ref):
    half = core_ref.shape[0] // 2
    rows = c_rows.shape[0]
    c_wide = jnp.concatenate([c_rows] * 3, axis=1)
    for p in range(0, half, 2):
        x = jnp.concatenate([core_ref[p], core_ref[p + half], core_ref[p + 1], core_ref[p + 1 + half]], axis=1)
        high = x.astype(jnp.bfloat16)
        rest = x - high.astype(jnp.float32)
        mid, low = split(rest)
        first = dot(c_wide, jnp.concatenate([high, mid, low], axis=0), NN)
        first_ref[pl.ds(p, rows, stride=half), :] = first[:, :128]
        first_ref[pl.ds(p + 1, rows, stride=half), :] = first[:, 128:]


def shares_of(slots, values_ref, until_ref, a_all, b_all, first_ref):
    half = a_all.shape[1] // 2
    sides = {}

    def begin(n):
        a, b = a_all[n], b_all[n].astype(jnp.bfloat16)
        none = jnp.zeros_like(b)
        b_top = jnp.concatenate([b, none], axis=1)
        b_low = jnp.concatenate([none, b], axis=1)
        b_wide = jnp.concatenate([b_top, b_low, b_top, b_low], axis=0)
        a_cols = jnp.concatenate([a, a], axis=0).T.astype(jnp.bfloat16)
        return b_wide, a_cols, until_ref[n].astype(jnp.bfloat16)

    def project(n, start, b_wide):
        rows = pl.ds(pl.multiple_of((n * BT + start) * half, CHUNK * half), CHUNK * half)
        second = dot(jnp.concatenate(split(first_ref[rows, :]), axis=1), b_wide, NN)
        high, low = split(second)
        columns = []
        for t in range(CHUNK):
            rows = slice(t * half, (t + 1) * half)
            columns.append(jnp.concatenate(
                [high[rows, :128], high[rows, 128:], low[rows, :128], low[rows, 128:]], axis=0))
        return jnp.concatenate(columns, axis=1)

    def impute(n, start, columns, a_cols, until):
        rebuilt = dot(a_cols, columns, NN).astype(jnp.bfloat16)
        return jnp.concatenate([
            jnp.where(jnp.bfloat16(start + t) < until, values_ref[n, start + t], rebuilt[:, t * 128:(t + 1) * 128])
            for t in range(CHUNK)], axis=1)

    turns = [(u, start) for start in range(0, BT, CHUNK) for u in range(len(slots))]
    columns, imputed, totals = {}, {}, {}
    for k in range(len(turns) + AHEAD + 1):
        if k < len(turns):
            u, start = turns[k]
            if u not in sides:
                sides[u] = begin(slots[u])
            columns[k] = project(slots[u], start, sides[u][0])
        j = k - AHEAD
        if 0 <= j < len(turns):
            u, start = turns[j]
            imputed[j] = impute(slots[u], start, columns[j], *sides[u][1:])
        j = k - AHEAD - 1
        if j >= 0:
            u, _ = turns[j]
            term = dot(columns.pop(j), imputed.pop(j), NT)
            totals[u] = totals[u] + term if u in totals else term
    return [totals[u][:2 * half] + totals[u][2 * half:] for u in range(len(slots))]


def step_kernel(n_src, n_dst, values_hbm, until_hbm, a_hbm, b_hbm, core_hbm, c_hbm, blocks_hbm, count_hbm,
                share_out, ids_out,
                c_ref, blocks_ref, count_ref, named, values, until, a_own, b_own, a_cut, b_cut, core, c_all, c_flat, ids_src, a_send, a_get, b_send, b_get, a_all, b_all,
                first, shares,
                in_sem, v_sem, c_send, c_recv, h_send, h_recv, i_send, i_recv, j_send, j_recv,
                as_sem, ar_sem, bs_sem, br_sem, s_send, s_recv):
    src, dst = lax.axis_index("src"), lax.axis_index("dst")
    slots = values.shape[0]
    each_a, each_b = a_own.shape[0], b_own.shape[0]
    src_blocks, dst_blocks = a_own.shape[1] // BI, b_own.shape[1] // BJ

    small = [
        pltpu.make_async_copy(blocks_hbm, blocks_ref, in_sem.at[6]),
        pltpu.make_async_copy(c_hbm, c_ref, in_sem.at[7]),
        pltpu.make_async_copy(count_hbm, count_ref, in_sem.at[8]),
    ]
    loads = [
        pltpu.make_async_copy(a_hbm, a_own, in_sem.at[0]),
        pltpu.make_async_copy(b_hbm, b_own, in_sem.at[1]),
        pltpu.make_async_copy(core_hbm, core, in_sem.at[2]),
        pltpu.make_async_copy(until_hbm, until, in_sem.at[3]),
    ]
    for copy in small + loads:
        copy.start()
    for n in range(slots):
        pltpu.make_async_copy(values_hbm.at[n], values.at[n], v_sem.at[n]).start()

    def src_peer(step):
        return (lax.rem(src + step, n_src), dst)

    def dst_peer(step):
        return (src, lax.rem(dst + step, n_dst))

    barrier = pltpu.get_barrier_semaphore()
    for step in range(1, n_dst):
        pl.semaphore_signal(barrier, inc=1, device_id=dst_peer(step), device_id_type=MESH)
    for step in range(1, n_src):
        pl.semaphore_signal(barrier, inc=1, device_id=src_peer(step), device_id_type=MESH)

    def remote(source, target, send, recv, peer):
        return pltpu.make_async_remote_copy(
            src_ref=source, dst_ref=target, send_sem=send, recv_sem=recv, device_id=peer, device_id_type=MESH)

    for copy in small:
        copy.wait()
    hours_own, rank_c = c_ref.shape
    c_all[src, dst] = jnp.concatenate(
        [c_ref[...].astype(jnp.float32), jnp.zeros((hours_own, 128 - rank_c), jnp.float32)], axis=1)
    for n in range(slots):
        named[0, n] = lax.rem(blocks_ref[0, n], src_blocks)
        named[1, n] = lax.rem(blocks_ref[1, n], dst_blocks)
        named[2, n] = blocks_ref[2, n]
        named[3, n] = count_ref[0]
    pl.semaphore_wait(barrier, n_dst - 1 + n_src - 1)

    hours, near, far = [], [], []
    for step in range(1, n_src):
        peer = src_peer(step)
        hours.append(remote(c_all.at[src, dst], c_all.at[src, dst], c_send.at[step - 1], c_recv.at[step - 1], peer))
        hours[-1].start()
        far.append(remote(named, ids_src.at[src], i_send.at[step - 1], i_recv.at[step - 1], peer))
        far[-1].start()
    for step in range(1, n_dst):
        near.append(remote(named, ids_out.at[dst], j_send.at[step - 1], j_recv.at[step - 1], dst_peer(step)))
        near[-1].start()
    own_ids = pltpu.make_async_copy(named, ids_out.at[dst], in_sem.at[4])
    own_ids.start()
    for copy in loads[:2]:
        copy.wait()

    for s in range(src_blocks):
        a_cut[s] = a_own[:, s * BI:(s + 1) * BI].astype(jnp.float32)
    for d in range(dst_blocks):
        b_cut[d] = b_own[:, d * BJ:(d + 1) * BJ].astype(jnp.float32)

    def a_blocks(ids):
        blocks = [a_cut[ids[0, n]] for n in range(slots)]
        return jnp.concatenate(blocks, axis=0).astype(jnp.bfloat16)

    def b_blocks(ids):
        blocks = [b_cut[ids[1, n]] for n in range(slots)]
        return jnp.concatenate(blocks, axis=0).astype(jnp.bfloat16)

    a_get[dst] = a_blocks(named)
    b_get[src] = b_blocks(named)

    for copy in hours:
        copy.wait()
    onward = []
    for step in range(1, n_dst):
        onward.append(remote(
            c_all.at[:, dst], c_all.at[:, dst], h_send.at[step - 1], h_recv.at[step - 1], dst_peer(step)))
        onward[-1].start()

    parts = []
    for step in reversed(range(1, n_src)):
        far[step - 1].wait()
        back = lax.rem(src + n_src - step, n_src)
        b_send[step - 1] = b_blocks(ids_src.at[back])
        parts.append(remote(b_send.at[step - 1], b_get.at[src], bs_sem.at[step - 1], br_sem.at[step - 1], (back, dst)))
        parts[-1].start()
    for step in range(1, n_dst):
        near[step - 1].wait()
        back = lax.rem(dst + n_dst - step, n_dst)
        a_send[step - 1] = a_blocks(ids_out.at[back])
        parts.append(remote(a_send.at[step - 1], a_get.at[dst], as_sem.at[step - 1], ar_sem.at[step - 1], (src, back)))
        parts[-1].start()

    for copy in onward:
        copy.wait()
    c_flat[...] = c_all[...].reshape(c_flat.shape)
    c_rows = jnp.concatenate([c_flat[blocks_ref[2, n]] for n in range(slots)], axis=0)
    loads[2].wait()
    project_hours(core, c_rows[:, :rank_c].astype(jnp.bfloat16), first)

    for copy in parts + [own_ids, loads[3]]:
        copy.wait()
    for p in range(n_src):
        part = b_get[p].astype(jnp.float32)
        for n in range(slots):
            b_all[n, p * each_b:(p + 1) * each_b, :] = part[n * each_b:(n + 1) * each_b]
    for q in range(n_dst):
        part = a_get[q].astype(jnp.float32)
        for n in range(slots):
            a_all[n, q * each_a:(q + 1) * each_a, :] = part[n * each_a:(n + 1) * each_a]

    together = math.gcd(slots, TOGETHER)

    def to_peer(turn, step):
        peer = lax.rem(dst + step, n_dst)
        part = pl.ds(turn * together, together)
        return remote(shares.at[peer, part], share_out.at[dst, part],
                      s_send.at[turn, step - 1], s_recv.at[turn, step - 1], (src, peer))

    def some_slots(turn, carry):
        ns = [turn * together + u for u in range(together)]
        for n in ns:
            pltpu.make_async_copy(values_hbm.at[n], values.at[n], v_sem.at[n]).wait()
        for n, share in zip(ns, shares_of(ns, values, until, a_all, b_all, first)):
            for q in range(n_dst):
                shares[q, n] = share[q * each_a:(q + 1) * each_a]
            share_out[dst, n] = shares[dst, n]
        for step in range(1, n_dst):
            to_peer(turn, step).start()
        return carry

    lax.fori_loop(0, slots // together, some_slots, 0)
    for turn in range(slots // together):
        for step in range(1, n_dst):
            to_peer(turn, step).wait()


def slot_shares(n_src, n_dst, values, until, blocks, count, a, b, c, core):
    slots = values.shape[0]
    rank_a, rank_c, rank_b = core.shape
    each_a, each_b = a.shape[0], b.shape[0]
    vmem = pl.BlockSpec(memory_space=pltpu.VMEM)
    smem = pl.BlockSpec(memory_space=pltpu.SMEM)
    hbm = pl.BlockSpec(memory_space=pltpu.HBM)
    dma = pltpu.SemaphoreType.DMA
    far, near = dma((n_src - 1,)), dma((n_dst - 1,))
    return pl.pallas_call(
        functools.partial(step_kernel, n_src, n_dst),
        out_shape=(
            jax.ShapeDtypeStruct((n_dst, slots, each_a, BI), jnp.float32),
            jax.ShapeDtypeStruct((n_dst, 4, slots), jnp.int32),
        ),
        in_specs=[hbm] * 8,
        out_specs=(vmem, smem),
        scratch_shapes=[
            pltpu.VMEM(c.shape, c.dtype),
            pltpu.SMEM(blocks.shape, blocks.dtype),
            pltpu.SMEM(count.shape, count.dtype),
            pltpu.SMEM((4, slots), blocks.dtype),
            pltpu.VMEM(values.shape, values.dtype),
            pltpu.VMEM(until.shape, until.dtype),
            pltpu.VMEM(a.shape, a.dtype),
            pltpu.VMEM(b.shape, b.dtype),
            pltpu.VMEM((a.shape[1] // BI, each_a, BI), jnp.float32),
            pltpu.VMEM((b.shape[1] // BJ, each_b, BJ), jnp.float32),
            pltpu.VMEM(core.shape, core.dtype),
            pltpu.VMEM((n_src, n_dst, c.shape[0], 128), jnp.float32),
            pltpu.VMEM((n_src * n_dst * c.shape[0] // BT, BT, 128), jnp.float32),
            pltpu.SMEM((n_src, 4, slots), jnp.int32),
            pltpu.VMEM((n_dst - 1, slots * each_a, BI), a.dtype),
            pltpu.VMEM((n_dst, slots * each_a, BI), a.dtype),
            pltpu.VMEM((n_src - 1, slots * each_b, BJ), b.dtype),
            pltpu.VMEM((n_src, slots * each_b, BJ), b.dtype),
            pltpu.VMEM((slots, rank_a, BI), jnp.float32),
            pltpu.VMEM((slots, rank_b, BJ), jnp.float32),
            pltpu.VMEM((slots * BT * rank_a // 2, 128), jnp.float32),
            pltpu.VMEM((n_dst, slots, each_a, BI), jnp.float32),
            dma((9,)), dma((slots,)), far, far, near, near, far, far, near, near,
            near, near, far, far, dma((slots, n_dst - 1)), dma((slots, n_dst - 1)),
        ],
        compiler_params=pltpu.CompilerParams(
            collective_id=0, has_side_effects=True, vmem_limit_bytes=64 * 2 ** 20),
        name="slot_shares",
    )(values, until, a, b, core, c, blocks, count)


def sum_kernel(ids_ref, share_ref, out_ref):
    out_ref[...] = jnp.zeros_like(out_ref)
    for q in range(share_ref.shape[0]):
        for n in range(share_ref.shape[1]):
            @pl.when(n < ids_ref[q, 3, 0])
            def _():
                column = pl.ds(pl.multiple_of(ids_ref[q, 0, n] * BI, BI), BI)
                out_ref[:, column] += share_ref[q, n]


def sum_shares(ids, shares, columns):
    vmem = pl.BlockSpec(memory_space=pltpu.VMEM)
    smem = pl.BlockSpec(memory_space=pltpu.SMEM)
    return pl.pallas_call(
        sum_kernel,
        out_shape=jax.ShapeDtypeStruct((shares.shape[2], columns), jnp.float32),
        in_specs=[smem, vmem],
        out_specs=vmem,
        compiler_params=pltpu.CompilerParams(vmem_limit_bytes=64 * 2 ** 20),
        name="sum_shares",
    )(ids, shares)


def on_device(n_src, n_dst, values, until, blocks, count, a_factor, b_factor, c_factor, core):
    shares, ids = slot_shares(
        n_src, n_dst, values, until, blocks.T, count, a_factor, b_factor, c_factor.T, core.transpose(0, 2, 1))
    return sum_shares(ids, shares, a_factor.shape[1])


def solution(mesh):
    return jax.shard_map(
        functools.partial(on_device, mesh.shape["src"], mesh.shape["dst"]),
        mesh=mesh,
        in_specs=(
            P(("src", "dst"), None, None, None),
            P(("src", "dst"), None, None),
            P(("src", "dst"), None),
            P(("src", "dst")),
            P("dst", "src"),
            P("src", "dst"),
            P(None, ("src", "dst")),
            P(),
        ),
        out_specs=P("dst", "src"),
        check_vma=False,
    )
```

```python
import functools
import math

import jax
import jax.numpy as jnp
from jax import lax
from jax.experimental import pallas as pl
from jax.experimental.pallas import tpu as pltpu
from jax.sharding import PartitionSpec as P

BI = 128
BJ = 128
BT = 32
CHUNK = 8
AHEAD = 2
TOGETHER = 4
MESH = pl.DeviceIdType.MESH
NN = ((1,), (0,))
NT = ((1,), (1,))


def dot(x, y, contract):
    return lax.dot_general(x, y, (contract, ((), ())), preferred_element_type=jnp.float32)


def split(x):
    high = x.astype(jnp.bfloat16)
    return high, (x - high.astype(jnp.float32)).astype(jnp.bfloat16)


def split_core(core_ref, parts_ref):
    half = core_ref.shape[0] // 2
    for p in range(0, half, 2):
        x = jnp.concatenate([core_ref[p], core_ref[p + half], core_ref[p + 1], core_ref[p + 1 + half]], axis=1)
        high = x.astype(jnp.bfloat16)
        mid, low = split(x - high.astype(jnp.float32))
        parts_ref[p // 2] = jnp.concatenate([high, mid, low], axis=0)


def project_hours(parts_ref, c_rows, first_ref):
    half = 2 * parts_ref.shape[0]
    rows = c_rows.shape[0]
    c_wide = jnp.concatenate([c_rows] * 3, axis=1)
    for p in range(0, half, 2):
        first = dot(c_wide, parts_ref[p // 2], NN)
        first_ref[pl.ds(p, rows, stride=half), :] = first[:, :128]
        first_ref[pl.ds(p + 1, rows, stride=half), :] = first[:, 128:]


def shares_of(slots, values_ref, until_ref, a_all, b_all, first_ref):
    half = a_all.shape[1] // 2
    sides = {}

    def begin(n):
        a, b = a_all[n], b_all[n].astype(jnp.bfloat16)
        none = jnp.zeros_like(b)
        b_top = jnp.concatenate([b, none], axis=1)
        b_low = jnp.concatenate([none, b], axis=1)
        b_wide = jnp.concatenate([b_top, b_low, b_top, b_low], axis=0)
        a_cols = jnp.concatenate([a, a], axis=0).T.astype(jnp.bfloat16)
        return b_wide, a_cols, until_ref[n].astype(jnp.bfloat16)

    def project(n, start, b_wide):
        rows = pl.ds(pl.multiple_of((n * BT + start) * half, CHUNK * half), CHUNK * half)
        second = dot(jnp.concatenate(split(first_ref[rows, :]), axis=1), b_wide, NN)
        high, low = split(second)
        columns = []
        for t in range(CHUNK):
            rows = slice(t * half, (t + 1) * half)
            columns.append(jnp.concatenate(
                [high[rows, :128], high[rows, 128:], low[rows, :128], low[rows, 128:]], axis=0))
        return jnp.concatenate(columns, axis=1)

    def impute(n, start, columns, a_cols, until):
        rebuilt = dot(a_cols, columns, NN).astype(jnp.bfloat16)
        return jnp.concatenate([
            jnp.where(jnp.bfloat16(start + t) < until, values_ref[n, start + t], rebuilt[:, t * 128:(t + 1) * 128])
            for t in range(CHUNK)], axis=1)

    turns = [(u, start) for start in range(0, BT, CHUNK) for u in range(len(slots))]
    columns, imputed, totals = {}, {}, {}
    for k in range(len(turns) + AHEAD + 1):
        if k < len(turns):
            u, start = turns[k]
            if u not in sides:
                sides[u] = begin(slots[u])
            columns[k] = project(slots[u], start, sides[u][0])
        j = k - AHEAD
        if 0 <= j < len(turns):
            u, start = turns[j]
            imputed[j] = impute(slots[u], start, columns[j], *sides[u][1:])
        j = k - AHEAD - 1
        if j >= 0:
            u, _ = turns[j]
            term = dot(columns.pop(j), imputed.pop(j), NT)
            totals[u] = totals[u] + term if u in totals else term
    return [totals[u][:2 * half] + totals[u][2 * half:] for u in range(len(slots))]


def step_kernel(n_src, n_dst, values_hbm, until_hbm, a_hbm, b_hbm, core_hbm, c_hbm, blocks_hbm, count_hbm,
                share_out, ids_out,
                c_ref, blocks_ref, count_ref, named, values, until, a_own, b_own, a_cut, b_cut, core, c_all, c_flat, ids_src, a_send, a_get, b_send, b_get, a_all, b_all,
                core_parts, first, shares,
                in_sem, v_sem, c_send, c_recv, h_send, h_recv, i_send, i_recv, j_send, j_recv,
                as_sem, ar_sem, bs_sem, br_sem, s_send, s_recv):
    src, dst = lax.axis_index("src"), lax.axis_index("dst")
    slots = values.shape[0]
    each_a, each_b = a_own.shape[0], b_own.shape[0]
    src_blocks, dst_blocks = a_own.shape[1] // BI, b_own.shape[1] // BJ

    small = [
        pltpu.make_async_copy(blocks_hbm, blocks_ref, in_sem.at[6]),
        pltpu.make_async_copy(c_hbm, c_ref, in_sem.at[7]),
        pltpu.make_async_copy(count_hbm, count_ref, in_sem.at[8]),
    ]
    loads = [
        pltpu.make_async_copy(a_hbm, a_own, in_sem.at[0]),
        pltpu.make_async_copy(b_hbm, b_own, in_sem.at[1]),
        pltpu.make_async_copy(core_hbm, core, in_sem.at[2]),
        pltpu.make_async_copy(until_hbm, until, in_sem.at[3]),
    ]
    for copy in small + loads:
        copy.start()
    for n in range(slots):
        pltpu.make_async_copy(values_hbm.at[n], values.at[n], v_sem.at[n]).start()

    def src_peer(step):
        return (lax.rem(src + step, n_src), dst)

    def dst_peer(step):
        return (src, lax.rem(dst + step, n_dst))

    barrier = pltpu.get_barrier_semaphore()
    for step in range(1, n_dst):
        pl.semaphore_signal(barrier, inc=1, device_id=dst_peer(step), device_id_type=MESH)
    for step in range(1, n_src):
        pl.semaphore_signal(barrier, inc=1, device_id=src_peer(step), device_id_type=MESH)

    def remote(source, target, send, recv, peer):
        return pltpu.make_async_remote_copy(
            src_ref=source, dst_ref=target, send_sem=send, recv_sem=recv, device_id=peer, device_id_type=MESH)

    for copy in small:
        copy.wait()
    hours_own, rank_c = c_ref.shape
    c_all[src, dst] = jnp.concatenate(
        [c_ref[...].astype(jnp.float32), jnp.zeros((hours_own, 128 - rank_c), jnp.float32)], axis=1)
    for n in range(slots):
        named[0, n] = lax.rem(blocks_ref[0, n], src_blocks)
        named[1, n] = lax.rem(blocks_ref[1, n], dst_blocks)
        named[2, n] = blocks_ref[2, n]
        named[3, n] = count_ref[0]
    pl.semaphore_wait(barrier, n_dst - 1 + n_src - 1)

    hours, near, far = [], [], []
    for step in range(1, n_src):
        peer = src_peer(step)
        hours.append(remote(c_all.at[src, dst], c_all.at[src, dst], c_send.at[step - 1], c_recv.at[step - 1], peer))
        hours[-1].start()
        far.append(remote(named, ids_src.at[src], i_send.at[step - 1], i_recv.at[step - 1], peer))
        far[-1].start()
    for step in range(1, n_dst):
        near.append(remote(named, ids_out.at[dst], j_send.at[step - 1], j_recv.at[step - 1], dst_peer(step)))
        near[-1].start()
    own_ids = pltpu.make_async_copy(named, ids_out.at[dst], in_sem.at[4])
    own_ids.start()
    for copy in loads[:2]:
        copy.wait()

    for s in range(src_blocks):
        a_cut[s] = a_own[:, s * BI:(s + 1) * BI].astype(jnp.float32)
    for d in range(dst_blocks):
        b_cut[d] = b_own[:, d * BJ:(d + 1) * BJ].astype(jnp.float32)

    def a_blocks(ids):
        blocks = [a_cut[ids[0, n]] for n in range(slots)]
        return jnp.concatenate(blocks, axis=0).astype(jnp.bfloat16)

    def b_blocks(ids):
        blocks = [b_cut[ids[1, n]] for n in range(slots)]
        return jnp.concatenate(blocks, axis=0).astype(jnp.bfloat16)

    a_get[dst] = a_blocks(named)
    b_get[src] = b_blocks(named)

    for copy in hours:
        copy.wait()
    onward = []
    for step in range(1, n_dst):
        onward.append(remote(
            c_all.at[:, dst], c_all.at[:, dst], h_send.at[step - 1], h_recv.at[step - 1], dst_peer(step)))
        onward[-1].start()

    parts = []
    for step in reversed(range(1, n_src)):
        far[step - 1].wait()
        back = lax.rem(src + n_src - step, n_src)
        b_send[step - 1] = b_blocks(ids_src.at[back])
        parts.append(remote(b_send.at[step - 1], b_get.at[src], bs_sem.at[step - 1], br_sem.at[step - 1], (back, dst)))
        parts[-1].start()
    for step in range(1, n_dst):
        near[step - 1].wait()
        back = lax.rem(dst + n_dst - step, n_dst)
        a_send[step - 1] = a_blocks(ids_out.at[back])
        parts.append(remote(a_send.at[step - 1], a_get.at[dst], as_sem.at[step - 1], ar_sem.at[step - 1], (src, back)))
        parts[-1].start()

    loads[2].wait()
    split_core(core, core_parts)
    for copy in onward:
        copy.wait()
    c_flat[...] = c_all[...].reshape(c_flat.shape)
    c_rows = jnp.concatenate([c_flat[blocks_ref[2, n]] for n in range(slots)], axis=0)
    project_hours(core_parts, c_rows[:, :rank_c].astype(jnp.bfloat16), first)

    for copy in parts + [own_ids, loads[3]]:
        copy.wait()
    for p in range(n_src):
        part = b_get[p].astype(jnp.float32)
        for n in range(slots):
            b_all[n, p * each_b:(p + 1) * each_b, :] = part[n * each_b:(n + 1) * each_b]
    for q in range(n_dst):
        part = a_get[q].astype(jnp.float32)
        for n in range(slots):
            a_all[n, q * each_a:(q + 1) * each_a, :] = part[n * each_a:(n + 1) * each_a]

    together = math.gcd(slots, TOGETHER)

    def to_peer(turn, step):
        peer = lax.rem(dst + step, n_dst)
        part = pl.ds(turn * together, together)
        return remote(shares.at[peer, part], share_out.at[dst, part],
                      s_send.at[turn, step - 1], s_recv.at[turn, step - 1], (src, peer))

    def some_slots(turn, carry):
        ns = [turn * together + u for u in range(together)]
        for n in ns:
            pltpu.make_async_copy(values_hbm.at[n], values.at[n], v_sem.at[n]).wait()
        for n, share in zip(ns, shares_of(ns, values, until, a_all, b_all, first)):
            for q in range(n_dst):
                shares[q, n] = share[q * each_a:(q + 1) * each_a]
            share_out[dst, n] = shares[dst, n]
        for step in range(1, n_dst):
            to_peer(turn, step).start()
        return carry

    lax.fori_loop(0, slots // together, some_slots, 0)
    for turn in range(slots // together):
        for step in range(1, n_dst):
            to_peer(turn, step).wait()


def slot_shares(n_src, n_dst, values, until, blocks, count, a, b, c, core):
    slots = values.shape[0]
    rank_a, rank_c, rank_b = core.shape
    each_a, each_b = a.shape[0], b.shape[0]
    vmem = pl.BlockSpec(memory_space=pltpu.VMEM)
    smem = pl.BlockSpec(memory_space=pltpu.SMEM)
    hbm = pl.BlockSpec(memory_space=pltpu.HBM)
    dma = pltpu.SemaphoreType.DMA
    far, near = dma((n_src - 1,)), dma((n_dst - 1,))
    return pl.pallas_call(
        functools.partial(step_kernel, n_src, n_dst),
        out_shape=(
            jax.ShapeDtypeStruct((n_dst, slots, each_a, BI), jnp.float32),
            jax.ShapeDtypeStruct((n_dst, 4, slots), jnp.int32),
        ),
        in_specs=[hbm] * 8,
        out_specs=(vmem, smem),
        scratch_shapes=[
            pltpu.VMEM(c.shape, c.dtype),
            pltpu.SMEM(blocks.shape, blocks.dtype),
            pltpu.SMEM(count.shape, count.dtype),
            pltpu.SMEM((4, slots), blocks.dtype),
            pltpu.VMEM(values.shape, values.dtype),
            pltpu.VMEM(until.shape, until.dtype),
            pltpu.VMEM(a.shape, a.dtype),
            pltpu.VMEM(b.shape, b.dtype),
            pltpu.VMEM((a.shape[1] // BI, each_a, BI), jnp.float32),
            pltpu.VMEM((b.shape[1] // BJ, each_b, BJ), jnp.float32),
            pltpu.VMEM(core.shape, core.dtype),
            pltpu.VMEM((n_src, n_dst, c.shape[0], 128), jnp.float32),
            pltpu.VMEM((n_src * n_dst * c.shape[0] // BT, BT, 128), jnp.float32),
            pltpu.SMEM((n_src, 4, slots), jnp.int32),
            pltpu.VMEM((n_dst - 1, slots * each_a, BI), a.dtype),
            pltpu.VMEM((n_dst, slots * each_a, BI), a.dtype),
            pltpu.VMEM((n_src - 1, slots * each_b, BJ), b.dtype),
            pltpu.VMEM((n_src, slots * each_b, BJ), b.dtype),
            pltpu.VMEM((slots, rank_a, BI), jnp.float32),
            pltpu.VMEM((slots, rank_b, BJ), jnp.float32),
            pltpu.VMEM((rank_a // 4, 3 * rank_c, 4 * rank_b), jnp.bfloat16),
            pltpu.VMEM((slots * BT * rank_a // 2, 128), jnp.float32),
            pltpu.VMEM((n_dst, slots, each_a, BI), jnp.float32),
            dma((9,)), dma((slots,)), far, far, near, near, far, far, near, near,
            near, near, far, far, dma((slots, n_dst - 1)), dma((slots, n_dst - 1)),
        ],
        compiler_params=pltpu.CompilerParams(
            collective_id=0, has_side_effects=True, vmem_limit_bytes=64 * 2 ** 20),
        name="slot_shares",
    )(values, until, a, b, core, c, blocks, count)


def sum_kernel(ids_ref, share_ref, out_ref):
    out_ref[...] = jnp.zeros_like(out_ref)
    for q in range(share_ref.shape[0]):
        for n in range(share_ref.shape[1]):
            @pl.when(n < ids_ref[q, 3, 0])
            def _():
                column = pl.ds(pl.multiple_of(ids_ref[q, 0, n] * BI, BI), BI)
                out_ref[:, column] += share_ref[q, n]


def sum_shares(ids, shares, columns):
    vmem = pl.BlockSpec(memory_space=pltpu.VMEM)
    smem = pl.BlockSpec(memory_space=pltpu.SMEM)
    return pl.pallas_call(
        sum_kernel,
        out_shape=jax.ShapeDtypeStruct((shares.shape[2], columns), jnp.float32),
        in_specs=[smem, vmem],
        out_specs=vmem,
        compiler_params=pltpu.CompilerParams(vmem_limit_bytes=64 * 2 ** 20),
        name="sum_shares",
    )(ids, shares)


def on_device(n_src, n_dst, values, until, blocks, count, a_factor, b_factor, c_factor, core):
    shares, ids = slot_shares(
        n_src, n_dst, values, until, blocks.T, count, a_factor, b_factor, c_factor.T, core.transpose(0, 2, 1))
    return sum_shares(ids, shares, a_factor.shape[1])


def solution(mesh):
    return jax.shard_map(
        functools.partial(on_device, mesh.shape["src"], mesh.shape["dst"]),
        mesh=mesh,
        in_specs=(
            P(("src", "dst"), None, None, None),
            P(("src", "dst"), None, None),
            P(("src", "dst"), None),
            P(("src", "dst")),
            P("dst", "src"),
            P("src", "dst"),
            P(None, ("src", "dst")),
            P(),
        ),
        out_specs=P("dst", "src"),
        check_vma=False,
    )
```
